256 devices in a mesh: slab: 64 (over x, z, core), tile: 4 (over y).
Axes of the slice: x: 4, y: 4, z: 8, core: 2. Of those that a mesh axis runs over, the one named last changes fastest.
Arguments:
- bricks: bfloat16 [64, 32, 32, 16, 256], P('slab', 'tile'), may hold values from -8 to 8
- send_list: int32 [64, 16, 2], P('slab', 'tile'), may hold values from -1 to 7, as said below
- sample_voxel: int32 [64, 512, 128], P('slab', 'tile'), may hold values from 0 to 3822, as said below
- sample_frac: float32 [64, 512, 3, 128], P('slab', 'tile'), may hold values from 0 to 1
- block_slot: int32 [64, 512], P('slab', 'tile'), may hold values from 0 to 7, as said below
- block_group: int32 [64, 512], P('slab', 'tile'), may hold values from -1 to 255, as said below
- density_weight: float32 [32], replicated, may hold values from -3 to 3
- background: float32 [32], replicated, may hold values from -4 to 4
- decode_weight: float32 [3, 32], replicated, may hold values from -2.1 to 2.1
- target: float32 [3, 4, 8192], P(None, 'tile', 'slab'), may hold values from 0 to 1
Outputs:
- rendered: float32 [3, 4, 8192], P(None, 'tile', 'slab')
- pixel_loss: float32 [4, 8192], P('tile', 'slab')
The draws below stay inside these ranges and needn't reach their ends.
Inputs may be any that keep to these rules, and one draw needn't show every extreme that they name: `send_list`: entry [s, u * 4 + d, k] is the local brick that device (slab s, tile u) puts in send slot k for tile owner d of its slab, or -1 for an empty slot; the filled slots of a list come first, name distinct bricks and number 1 to 2; in every slab some owner gets 2 bricks from every source. `block_slot`: block b of owner (s, t) reads slot u * 2 + k, a filled slot of the list that tile u of slab s sends to t, where u = b // 32: a device's blocks come in 4 runs by source; every filled slot is read by some filled block of its run. `block_group`: -1 marks an empty block; in each run the filled blocks come first, all runs of a device hold the same number of filled blocks, at least 2, and a device's filled blocks have distinct groups; in every tile some slab's device is full. `sample_voxel`: x * 16 * 16 + y * 16 + z with x, y, z each at most 14.
All inputs are finite; a program needn't handle non-finite values.
Results may differ from the reference program's by a relative error of at most 0.0033.
Values may be sent and summed in bfloat16 or wider, within the bound.
No kernel may reach another device: no remote copies, remote signals or barrier semaphores. Data moves between devices by JAX's collectives and lax.ppermute only.
A program may use at most 64 MiB of HBM per device.

```python
import jax
import jax.numpy as jnp
from jax import lax

C = 32
EDGE = 16
SAMP = 128
SPR = 4
NBLK = 128
BRICK_DEV = 8
CAP = 2
RPB = 32
GROUPS = 256
RAYS_T = 8192
N_SLAB = 64
N_TILE = 4


def routing_counts(key):
    base_key = jax.random.fold_in(key, 7001)
    counts = jax.random.randint(jax.random.fold_in(base_key, 1), (N_SLAB, N_TILE, N_TILE), 1, CAP + 1)
    full_owner = jax.random.randint(jax.random.fold_in(base_key, 2), (N_SLAB, 1, 1), 0, N_TILE)
    owner_row = jnp.arange(N_TILE, dtype=jnp.int32).reshape(1, 1, N_TILE)
    return jnp.where(owner_row == full_owner, CAP, counts).astype(jnp.int32)


def fill_counts(key):
    base_key = jax.random.fold_in(key, 7201)
    levels = jax.random.randint(jax.random.fold_in(base_key, 1), (N_SLAB, N_TILE), 0, 4)
    full_slab = jax.random.randint(jax.random.fold_in(base_key, 2), (1, N_TILE), 0, N_SLAB)
    slab_row = jnp.arange(N_SLAB, dtype=jnp.int32)[:, None]
    levels = jnp.where(slab_row == full_slab, 0, levels)
    return jnp.maximum(NBLK // N_TILE // (1 + levels), CAP).astype(jnp.int32)


def draw_send_list(key, part):
    counts = routing_counts(key)
    scores = jax.random.randint(jax.random.fold_in(key, 7002), (N_SLAB, N_TILE, N_TILE, BRICK_DEV), 0, 1 << 20)
    scores = scores * BRICK_DEV + jnp.arange(BRICK_DEV, dtype=jnp.int32)
    brick_order = jnp.argsort(scores, axis=-1)[..., :CAP].astype(jnp.int32)
    slot_index = jnp.arange(CAP, dtype=jnp.int32)
    send_lists = jnp.where(slot_index < counts[..., None], brick_order, -1)
    return send_lists.reshape(N_SLAB, N_TILE * N_TILE, CAP).astype(jnp.int32)


def draw_block_slot(key, part):
    counts = routing_counts(key)
    run_length = NBLK // N_TILE
    count_rows = jnp.repeat(jnp.transpose(counts, (0, 2, 1)), run_length, axis=2)
    position_in_run = jnp.tile(jnp.arange(run_length, dtype=jnp.int32), N_TILE)[None, None, :]
    offsets = jax.random.randint(jax.random.fold_in(key, 7003), (N_SLAB, N_TILE, N_TILE), 0, jnp.transpose(counts, (0, 2, 1)))
    offset_rows = jnp.repeat(offsets, run_length, axis=2)
    picked = jax.random.randint(jax.random.fold_in(key, 7004), (N_SLAB, N_TILE, NBLK), 0, count_rows)
    chosen_slot = jnp.where(position_in_run < count_rows, (position_in_run + offset_rows) % count_rows, picked)
    source_tile = (jnp.arange(NBLK, dtype=jnp.int32) // run_length)[None, None, :]
    return (source_tile * CAP + chosen_slot).reshape(N_SLAB, N_TILE * NBLK).astype(jnp.int32)


def draw_block_group(key, part):
    filled = fill_counts(key)
    scores = jax.random.randint(jax.random.fold_in(key, 7202), (N_SLAB, N_TILE, GROUPS), 0, 1 << 20)
    scores = scores * GROUPS + jnp.arange(GROUPS, dtype=jnp.int32)
    group_order = jnp.argsort(scores, axis=-1)[..., :NBLK].astype(jnp.int32)
    position_in_run = jnp.tile(jnp.arange(NBLK // N_TILE, dtype=jnp.int32), N_TILE)[None, None, :]
    chosen = jnp.where(position_in_run < filled[..., None], group_order, -1)
    return chosen.reshape(N_SLAB, N_TILE * NBLK).astype(jnp.int32)


def draw_sample_voxel(key, part):
    shape_all = (N_SLAB, N_TILE * NBLK, SAMP)
    coords = jax.random.randint(jax.random.fold_in(key, 7101), (3,) + shape_all, 0, EDGE - 1)
    return (coords[0] * EDGE * EDGE + coords[1] * EDGE + coords[2]).astype(jnp.int32)


def block_levels(stream_key, extent, cuts, smallest, high):
    gain = 1.0
    for dim, blocks in cuts:
        draws = jax.random.uniform(jax.random.fold_in(jax.random.fold_in(stream_key, 6), dim), (blocks,), jnp.float32, smallest / len(cuts), high / len(cuts))
        gain = gain * jnp.repeat(jnp.exp(draws), extent[dim] // blocks).reshape((-1,) + (1,) * (len(extent) - 1 - dim))
    return gain


def scatter_about(rng, dims, width, bound, pieces=(), kind=jnp.bfloat16):
    gain = block_levels(rng, dims, pieces, -0.22, 0.18) if pieces else 1.0
    array = jax.random.normal(rng, dims, jnp.float32) * width * gain
    return jnp.minimum(jnp.maximum(array, -bound), bound).astype(kind)


def setup_inputs(seed: int = 0) -> dict:
    arg_keys = jax.random.split(jax.random.key(seed), 11)
    return {
        "bricks": scatter_about(arg_keys[0], (N_SLAB, N_TILE * BRICK_DEV, C, EDGE, EDGE * EDGE), 1.5, 8.0, ((0, 64), (1, 4))),
        "send_list": draw_send_list(jax.random.fold_in(arg_keys[10], 71), 0),
        "sample_voxel": draw_sample_voxel(jax.random.fold_in(arg_keys[10], 71), 0),
        "sample_frac": jnp.clip(1.0 * jax.random.uniform(arg_keys[3], (N_SLAB, N_TILE * NBLK, 3, SAMP), jnp.float32) ** block_levels(arg_keys[3], (N_SLAB, N_TILE * NBLK, 3, SAMP), ((0, 64), (1, 4)), -0.2, 0.2), 0.0, 1.0),
        "block_slot": draw_block_slot(jax.random.fold_in(arg_keys[10], 71), 0),
        "block_group": draw_block_group(jax.random.fold_in(arg_keys[10], 71), 0),
        "density_weight": scatter_about(arg_keys[6], (C,), 0.5, 3.0, (), jnp.float32),
        "background": scatter_about(arg_keys[7], (C,), 1.0, 4.0, (), jnp.float32),
        "decode_weight": scatter_about(arg_keys[8], (3, C), 0.7, 2.1, (), jnp.float32),
        "target": jnp.clip(1.0 * jax.random.uniform(arg_keys[9], (3, N_TILE, RAYS_T), jnp.float32) ** block_levels(arg_keys[9], (3, N_TILE, RAYS_T), ((1, 4), (2, 64)), -0.2, 0.2), 0.0, 1.0),
    }


step_length = 0.02


def gather_features(brick_store, brick_ids, base_voxel, fractions):
    brick_edge = brick_store.shape[2]
    channels = brick_store.shape[1]
    cell_x = base_voxel // (brick_edge * brick_edge)
    cell_y = (base_voxel // brick_edge) % brick_edge
    cell_z = base_voxel % brick_edge
    frac_x = fractions[:, 0]
    frac_y = fractions[:, 1]
    frac_z = fractions[:, 2]
    chan_index = jnp.arange(channels, dtype=jnp.int32)[None, :, None]
    brick_index = brick_ids.astype(jnp.int32)[:, None, None]
    plane_sums = []
    for offset_x in (0, 1):
        plane_sum = jnp.zeros((base_voxel.shape[0], channels, base_voxel.shape[1]), jnp.float32)
        for offset_y in (0, 1):
            for offset_z in (0, 1):
                weight_y = frac_y if offset_y == 1 else 1.0 - frac_y
                weight_z = frac_z if offset_z == 1 else 1.0 - frac_z
                rounded = lax.optimization_barrier((weight_y * weight_z).astype(jnp.bfloat16))
                row_index = (cell_x + offset_x).astype(jnp.int32)[:, None, :]
                column_index = ((cell_y + offset_y) * brick_edge + cell_z + offset_z).astype(jnp.int32)[:, None, :]
                values = brick_store[brick_index, chan_index, row_index, column_index].astype(jnp.float32)
                plane_sum = plane_sum + rounded.astype(jnp.float32)[:, None, :] * values
        plane_sums.append(plane_sum)
    blended = (1.0 - frac_x)[:, None, :] * plane_sums[0] + frac_x[:, None, :] * plane_sums[1]
    return blended.astype(jnp.bfloat16)


def shade_blocks(features, density_weight):
    blocks = features.shape[0]
    channels = features.shape[1]
    samples = features.astype(jnp.float32).reshape(blocks, channels, SPR, -1)
    logits = jnp.einsum("c,bcsr->bsr", density_weight.astype(jnp.float32), samples, precision=lax.Precision.HIGHEST)
    density = jax.nn.softplus(logits)
    opacity = 1.0 - jnp.exp(-step_length * density)
    through = jnp.cumprod(1.0 - opacity, axis=1)
    before = jnp.concatenate([jnp.ones_like(through[:, :1]), through[:, :-1]], axis=1)
    block_feature = jnp.einsum("bsr,bcsr->bcr", before * opacity, samples, precision=lax.Precision.HIGHEST)
    return block_feature, through[:, -1]


def reference(bricks, send_list, sample_voxel, sample_frac, block_slot, block_group, density_weight, background, decode_weight, target):
    block_tile = jnp.arange(N_TILE * NBLK, dtype=jnp.int32) // NBLK

    def slab_step(carry, inputs):
        front_feature, front_pass = carry
        slab_bricks, slab_lists, slab_voxel, slab_frac, slab_slot, slab_group = inputs
        source = slab_slot // CAP
        position = slab_slot % CAP
        local_ids = slab_lists[source * N_TILE + block_tile, position]
        brick_ids = source * BRICK_DEV + local_ids
        features = gather_features(slab_bricks, brick_ids, slab_voxel, slab_frac)
        block_feature, block_pass = shade_blocks(features, density_weight)
        dest_row = jnp.where(slab_group >= 0, block_tile * GROUPS + slab_group, N_TILE * GROUPS).astype(jnp.int32)
        slab_feature = jnp.zeros((N_TILE * GROUPS, C, RPB), jnp.float32).at[dest_row].set(block_feature, mode="drop")
        slab_pass = jnp.ones((N_TILE * GROUPS, RPB), jnp.float32).at[dest_row].set(block_pass, mode="drop")
        slab_feature = slab_feature.reshape(N_TILE, GROUPS, C, RPB).transpose(2, 0, 1, 3).reshape(C, N_TILE, RAYS_T)
        slab_pass = slab_pass.reshape(N_TILE, RAYS_T)
        return (front_feature + front_pass[None] * slab_feature, front_pass * slab_pass), None

    start = (jnp.zeros((C, N_TILE, RAYS_T), jnp.float32), jnp.ones((N_TILE, RAYS_T), jnp.float32))
    totals, unused = lax.scan(slab_step, start, (bricks, send_list, sample_voxel, sample_frac, block_slot, block_group))
    total_feature, total_pass = totals
    final_feature = total_feature + total_pass[None] * background.astype(jnp.float32)[:, None, None]
    logits = jnp.einsum("kc,ctr->ktr", decode_weight, final_feature, precision=lax.Precision.HIGHEST)
    rendered = jax.nn.sigmoid(logits)
    difference = rendered - target
    pixel_loss = jnp.sum(difference * difference, axis=0)
    return rendered, pixel_loss
```

```python
import jax
import jax.numpy as jnp
from jax import lax
from jax.experimental import pallas as pl
from jax.experimental.pallas import tpu as pltpu
from jax.sharding import PartitionSpec as P

SPR = 4
GROUPS = 256
VALUES = 4

step_length = 0.02
f32 = jnp.float32
bf16 = jnp.bfloat16


def whole(space):
    return pl.BlockSpec(memory_space=space)


def decode_kernel(send_ref, density_ref, decode_ref, bricks_ref, out_ref, buffer, sems):
    slots = out_ref.shape[0]
    capacity = send_ref.shape[1]
    last_brick = bricks_ref.shape[1] - 1
    channels, edge, plane = bricks_ref.shape[2:]

    def copy_of(slot):
        brick = jnp.clip(send_ref[0, slot % capacity, slot // capacity], 0, last_brick)
        return pltpu.make_async_copy(bricks_ref.at[0, brick], buffer.at[slot], sems.at[slot])

    for slot in range(slots):
        copy_of(slot).start()

    def one_slot(slot, carry):
        copy_of(slot).wait()
        sums = [jnp.zeros((edge, plane), f32) for _ in range(VALUES)]
        for c in range(channels):
            values = buffer[slot, c].astype(f32)
            weights = [density_ref[c]] + [decode_ref[k, c] for k in range(VALUES - 1)]
            sums = [total + weight * values for total, weight in zip(sums, weights)]
        for k in range(VALUES):
            out_ref[slot, k * edge : (k + 1) * edge, :] = sums[k].astype(bf16)
        return carry

    lax.fori_loop(0, slots, one_slot, 0)


def decode_bricks(send_list, density_weight, decode_weight, bricks):
    slots = send_list.shape[1] * send_list.shape[2]
    channels, edge, plane = bricks.shape[2:]
    return pl.pallas_call(
        decode_kernel,
        out_shape=jax.ShapeDtypeStruct((slots, VALUES * edge, plane), bf16),
        in_specs=[whole(pltpu.SMEM)] * 3 + [whole(pltpu.HBM)],
        out_specs=whole(pltpu.VMEM),
        scratch_shapes=[
            pltpu.VMEM((slots, channels, edge, plane), bf16),
            pltpu.SemaphoreType.DMA((slots,)),
        ],
        compiler_params=pltpu.CompilerParams(vmem_limit_bytes=8 << 20),
        name="decode_bricks",
    )(send_list.transpose(0, 2, 1), density_weight, decode_weight, bricks)


def hat(position, line):
    return jnp.maximum(1.0 - jnp.abs(position - line), 0.0)


def sum_rows(parts):
    row = lax.broadcasted_iota(jnp.int32, parts[0].shape, 0)
    halves = []
    for j in range(4):
        low, high = parts[j], parts[j + 4]
        kept = jnp.where(row < 4, low, high)
        moved = jnp.where(row < 4, high, low)
        both = kept + pltpu.roll(moved, 4, 0)
        both = both + pltpu.roll(both, 1 if j & 1 else 7, 0)
        both = both + pltpu.roll(both, 2 if j & 2 else 6, 0)
        halves.append(both)
    odd = (row & 1) == 1
    pair0 = jnp.where(odd, halves[1], halves[0])
    pair1 = jnp.where(odd, halves[3], halves[2])
    return jnp.where((row & 2) == 2, pair1, pair0)


def sample_kernel(slot_ref, planes_ref, voxel_ref, frac_ref, group_ref, column_ref, out_ref, shaded):
    blocks, samples = voxel_ref.shape[1:]
    edge = planes_ref.shape[1] // VALUES
    rays = samples // SPR
    batch = 8
    line = lax.broadcasted_iota(jnp.int32, (edge, samples), 0).astype(f32)
    lane = lax.broadcasted_iota(jnp.int32, (batch, samples), 1)
    quarter = lane // rays

    def one_batch(step, carry):
        first = pl.multiple_of(step * batch, batch)
        voxel = voxel_ref[0, pl.ds(first, batch), :]
        cells = (voxel // (edge * edge), voxel // edge % edge, voxel % edge)
        at_x, at_y, at_z = [
            cell.astype(f32) + frac_ref[0, axis, pl.ds(first, batch), :] for axis, cell in enumerate(cells)
        ]
        parts = []
        for j in range(batch):
            weight_x = hat(at_x[j : j + 1], line)
            weight_y = hat(at_y[j : j + 1], line)
            weight_z = hat(at_z[j : j + 1], line)
            plane_weights = (
                (weight_y[:, None, :] * weight_z[None, :, :]).reshape(edge * edge, samples).astype(bf16)
            )
            sums = jnp.dot(
                planes_ref[slot_ref[0, first + j]], plane_weights, preferred_element_type=f32
            )
            sums = sums.reshape(VALUES, edge // 8, 8, samples)
            parts.append(jnp.sum(sums * weight_x.reshape(1, edge // 8, 8, samples), axis=1))
        logit, red, green, blue = [sum_rows([part[k] for part in parts]) for k in range(VALUES)]
        depth = step_length * (jnp.maximum(logit, 0.0) + jnp.log1p(jnp.exp(-jnp.abs(logit))))
        before = jnp.zeros_like(depth)
        total = depth
        for d in range(1, SPR):
            moved = pltpu.roll(depth, d * rays, 1)
            before = before + jnp.where(quarter >= d, moved, 0.0)
            total = total + moved
        weight = jnp.exp(-before) * (1.0 - jnp.exp(-depth))
        place = quarter == column_ref[pl.ds(first, batch), :] % SPR
        for k, value in enumerate((red, green, blue)):
            value = weight * value
            value = value + pltpu.roll(value, 2 * rays, 1)
            value = value + pltpu.roll(value, rays, 1)
            shaded[k, pl.ds(first, batch), :] = jnp.where(place, value, 0.0)
        shaded[VALUES - 1, pl.ds(first, batch), :] = jnp.where(place, total, 0.0)
        return carry

    lax.fori_loop(0, blocks // batch, one_batch, 0)
    rows = out_ref.shape[0]
    row = lax.broadcasted_iota(jnp.int32, (rows, blocks), 0)
    home = group_ref[...] // SPR
    chosen = [
        ((home == row // VALUES) & (row % VALUES == k)).astype(f32).astype(bf16) for k in range(VALUES)
    ]
    placed = jnp.dot(
        jnp.concatenate(chosen, axis=1),
        shaded[...].astype(bf16).reshape(VALUES * blocks, samples),
        preferred_element_type=f32,
    )
    out_ref[...] = placed.astype(bf16)


def sample_and_place(block_slot, planes, sample_voxel, sample_frac, block_group):
    blocks, samples = sample_voxel.shape[1:]
    return pl.pallas_call(
        sample_kernel,
        out_shape=jax.ShapeDtypeStruct((GROUPS // SPR * VALUES, samples), bf16),
        in_specs=[whole(pltpu.SMEM)] + [whole(pltpu.VMEM)] * 5,
        out_specs=whole(pltpu.VMEM),
        scratch_shapes=[pltpu.VMEM((VALUES, blocks, samples), f32)],
        compiler_params=pltpu.CompilerParams(vmem_limit_bytes=8 << 20),
        name="sample_and_place",
    )(
        block_slot,
        planes,
        sample_voxel,
        sample_frac.transpose(0, 2, 1, 3),
        block_group,
        block_group.reshape(blocks, 1),
    )


def composite_kernel(got_ref, background_ref, decode_ref, target_ref, colour_ref, loss_ref):
    rows, rays = got_ref.shape
    got = got_ref[...]
    here = lax.broadcasted_iota(jnp.int32, (rows, rows), 0) // VALUES
    there = lax.broadcasted_iota(jnp.int32, (rows, rows), 1)
    nearer = (there // VALUES < here) & (there % VALUES == VALUES - 1)
    depth = jnp.dot(nearer.astype(f32).astype(bf16), got, preferred_element_type=f32)
    is_depth = lax.broadcasted_iota(jnp.int32, (rows, rays), 0) % VALUES == VALUES - 1
    terms = got.astype(f32) * jnp.where(is_depth, 1.0, jnp.exp(-depth))
    total = jnp.sum(terms.reshape(rows // 8, 8, rays), axis=0)
    total = total + pltpu.roll(total, VALUES, 0)
    behind = jnp.sum(decode_ref[...] * background_ref[...], axis=1, keepdims=True)
    logits = total[0:3] + jnp.exp(-total[3:4]) * behind
    colour = jax.nn.sigmoid(logits)
    difference = colour - target_ref[:, 0, :]
    colour_ref[:, 0, :] = colour
    loss_ref[...] = jnp.sum(difference * difference, axis=0, keepdims=True)


def composite(got, background, decode_weight, target):
    rays = got.shape[1]
    return pl.pallas_call(
        composite_kernel,
        out_shape=(
            jax.ShapeDtypeStruct((3, 1, rays), f32),
            jax.ShapeDtypeStruct((1, rays), f32),
        ),
        in_specs=[whole(pltpu.VMEM)] * 4,
        out_specs=(whole(pltpu.VMEM), whole(pltpu.VMEM)),
        compiler_params=pltpu.CompilerParams(vmem_limit_bytes=8 << 20),
        name="composite",
    )(got, background.reshape(1, -1), decode_weight, target)


def on_device(
    bricks,
    send_list,
    sample_voxel,
    sample_frac,
    block_slot,
    block_group,
    density_weight,
    background,
    decode_weight,
    target,
):
    slab_count = lax.axis_size("slab")
    planes = decode_bricks(send_list, density_weight, decode_weight, bricks)
    planes = lax.all_to_all(planes, "tile", split_axis=0, concat_axis=0, tiled=True)
    placed = sample_and_place(block_slot, planes, sample_voxel, sample_frac, block_group)
    placed = placed.reshape(slab_count, VALUES, placed.shape[1])
    got = lax.all_to_all(placed, "slab", split_axis=0, concat_axis=0, tiled=True)
    return composite(got.reshape(-1, got.shape[2]), background, decode_weight, target)


def solution(mesh):
    in_specs = (
        P("slab", "tile", None, None, None),
        P("slab", "tile", None),
        P("slab", "tile", None),
        P("slab", "tile", None, None),
        P("slab", "tile"),
        P("slab", "tile"),
        P(),
        P(),
        P(),
        P(None, "tile", "slab"),
    )
    out_specs = (P(None, "tile", "slab"), P("tile", "slab"))
    return jax.shard_map(
        on_device, mesh=mesh, in_specs=in_specs, out_specs=out_specs, check_vma=False
    )
```

```python
import functools

import jax
import jax.numpy as jnp
from jax import lax
from jax.experimental import pallas as pl
from jax.experimental.pallas import tpu as pltpu
from jax.sharding import PartitionSpec as P

SPR = 4
GROUPS = 256
VALUES = 4

step_length = 0.02
f32 = jnp.float32
bf16 = jnp.bfloat16


def whole(space):
    return pl.BlockSpec(memory_space=space)


def decode_kernel(send_ref, density_ref, decode_ref, bricks_ref, *refs):
    tiles = len(refs) - 6
    outs = refs[:tiles]
    send, density, decode, buffer, decoded, sems = refs[tiles:]
    capacity = outs[0].shape[0]
    bricks, channels, edge, plane = bricks_ref.shape[1:]
    small = [
        pltpu.make_async_copy(source, target, sems.at[bricks + i])
        for i, (source, target) in enumerate(
            ((send_ref, send), (density_ref, density), (decode_ref, decode))
        )
    ]
    large = [
        pltpu.make_async_copy(bricks_ref.at[0, brick], buffer.at[brick], sems.at[brick])
        for brick in range(bricks)
    ]
    for copy in small + large:
        copy.start()
    for copy in small:
        copy.wait()

    def one_brick(brick, carry):
        pltpu.make_async_copy(bricks_ref.at[0, brick], buffer.at[brick], sems.at[brick]).wait()
        sums = [jnp.zeros((edge, plane), f32) for _ in range(VALUES)]
        for c in range(channels):
            values = buffer[brick, c].astype(f32)
            weights = [density[c]] + [decode[k, c] for k in range(VALUES - 1)]
            sums = [total + weight * values for total, weight in zip(sums, weights)]
        for k in range(VALUES):
            decoded[brick, k * edge : (k + 1) * edge, :] = sums[k].astype(bf16)
        return carry

    lax.fori_loop(0, bricks, one_brick, 0)
    here = lax.axis_index("tile")
    for r in range(tiles):
        owner = lax.rem(here + r, tiles)
        for slot in range(capacity):
            outs[r][slot] = decoded[jnp.clip(send[0, slot, owner], 0, bricks - 1)]


def decode_bricks(send_list, density_weight, decode_weight, bricks):
    tiles, capacity = send_list.shape[1:]
    send_list = send_list.transpose(0, 2, 1)
    count, channels, edge, plane = bricks.shape[1:]
    return pl.pallas_call(
        decode_kernel,
        out_shape=(jax.ShapeDtypeStruct((capacity, VALUES * edge, plane), bf16),) * tiles,
        in_specs=[whole(pltpu.HBM)] * 4,
        out_specs=(whole(pltpu.VMEM),) * tiles,
        scratch_shapes=[
            pltpu.SMEM(send_list.shape, jnp.int32),
            pltpu.SMEM(density_weight.shape, f32),
            pltpu.SMEM(decode_weight.shape, f32),
            pltpu.VMEM((count, channels, edge, plane), bf16),
            pltpu.VMEM((count, VALUES * edge, plane), bf16),
            pltpu.SemaphoreType.DMA((count + 3,)),
        ],
        name="decode_bricks",
    )(send_list, density_weight, decode_weight, bricks)


def hat(position, line):
    return jnp.maximum(1.0 - jnp.abs(position - line), 0.0)


def sum_rows(parts):
    row = lax.broadcasted_iota(jnp.int32, parts[0].shape, 0)
    halves = []
    for j in range(4):
        low, high = parts[j], parts[j + 4]
        kept = jnp.where(row < 4, low, high)
        moved = jnp.where(row < 4, high, low)
        both = kept + pltpu.roll(moved, 4, 0)
        both = both + pltpu.roll(both, 1 if j & 1 else 7, 0)
        both = both + pltpu.roll(both, 2 if j & 2 else 6, 0)
        halves.append(both)
    odd = (row & 1) == 1
    pair0 = jnp.where(odd, halves[1], halves[0])
    pair1 = jnp.where(odd, halves[3], halves[2])
    return jnp.where((row & 2) == 2, pair1, pair0)


def sample_run(r, tiles, slot_ref, planes_ref, voxel_ref, frac_ref, column_ref, sampled, shaded, base):
    blocks, samples = voxel_ref.shape[1:]
    capacity = planes_ref.shape[0]
    edge = planes_ref.shape[1] // VALUES
    rays = samples // SPR
    run = blocks // tiles
    batch = 8
    bits = edge.bit_length() - 1
    line = lax.broadcasted_iota(jnp.int32, (edge, samples), 0).astype(f32)
    start = lax.rem(lax.axis_index("tile") + (tiles - r), tiles) * run

    def one_batch(step, carry):
        first = pl.multiple_of(start + step * batch, batch)
        voxel = voxel_ref[0, pl.ds(first, batch), :]
        cells = (voxel >> 2 * bits, (voxel >> bits) & (edge - 1), voxel & (edge - 1))
        at_x, at_y, at_z = [
            cell.astype(f32) + frac_ref[0, axis, pl.ds(first, batch), :] for axis, cell in enumerate(cells)
        ]
        parts = []
        for j in range(batch):
            weight_x = hat(at_x[j : j + 1], line)
            weight_y = hat(at_y[j : j + 1], line)
            weight_z = hat(at_z[j : j + 1], line)
            plane_weights = (
                (weight_y[:, None, :] * weight_z[None, :, :]).reshape(edge * edge, samples).astype(bf16)
            )
            slot = lax.rem(slot_ref[0, first + j], capacity)
            sums = jnp.dot(planes_ref[slot], plane_weights, preferred_element_type=f32)
            sums = sums.reshape(VALUES, edge // 8, 8, samples)
            parts.append(jnp.sum(sums * weight_x.reshape(1, edge // 8, 8, samples), axis=1))
        place = pl.multiple_of(step * batch, batch)
        for k in range(VALUES):
            sampled[k, pl.ds(place, batch), :] = sum_rows([part[k] for part in parts])
        return carry

    lax.fori_loop(0, run // batch, one_batch, 0, unroll=2)
    quarter = lax.broadcasted_iota(jnp.int32, (run, samples), 1) // rays
    rows = pl.ds(pl.multiple_of(start if base is None else base, run), run)
    logit = sampled[0]
    depth = step_length * (jnp.maximum(logit, 0.0) + jnp.log1p(jnp.exp(-jnp.abs(logit))))
    before = jnp.zeros_like(depth)
    total = depth
    for d in range(1, SPR):
        moved = pltpu.roll(depth, d * rays, 1)
        before = before + jnp.where(quarter >= d, moved, 0.0)
        total = total + moved
    weight = jnp.exp(-before) * (1.0 - jnp.exp(-depth))
    placed = quarter == (column_ref[pl.ds(pl.multiple_of(start, run), run), :] & (SPR - 1))
    for k in range(VALUES - 1):
        value = weight * sampled[k + 1]
        value = value + pltpu.roll(value, 2 * rays, 1)
        value = value + pltpu.roll(value, rays, 1)
        shaded[k, rows, :] = jnp.where(placed, value, 0.0).astype(bf16)
    shaded[VALUES - 1, rows, :] = jnp.where(placed, total, 0.0).astype(bf16)


def early_kernel(turns, tiles, slot_ref, voxel_ref, frac_ref, column_ref, *refs):
    planes, (out_ref, sampled) = refs[: len(turns)], refs[len(turns) :]
    run = voxel_ref.shape[1] // tiles
    for i, r in enumerate(turns):
        sample_run(
            r, tiles, slot_ref, planes[i], voxel_ref, frac_ref, column_ref, sampled, out_ref, i * run
        )


def sample_early(turns, tiles, blocks_in, planes):
    blocks, samples = blocks_in[1].shape[1:]
    run = blocks // tiles
    return pl.pallas_call(
        functools.partial(early_kernel, turns, tiles),
        out_shape=jax.ShapeDtypeStruct((VALUES, len(turns) * run, samples), bf16),
        in_specs=[whole(pltpu.SMEM)] + [whole(pltpu.VMEM)] * (3 + len(turns)),
        out_specs=whole(pltpu.VMEM),
        scratch_shapes=[pltpu.VMEM((VALUES, run, samples), f32)],
        compiler_params=pltpu.CompilerParams(vmem_limit_bytes=8 << 20),
        name="sample_early",
    )(*blocks_in, *planes)


def last_kernel(turns, tiles, slot_ref, voxel_ref, frac_ref, column_ref, group_ref, *refs):
    early = refs[: len(turns) - 1]
    planes_ref, out_ref, sampled, shaded = refs[len(turns) - 1 :]
    blocks, samples = voxel_ref.shape[1:]
    run = blocks // tiles
    for done, ref in zip(turns, early):
        for i, r in enumerate(done):
            start = lax.rem(lax.axis_index("tile") + (tiles - r), tiles) * run
            shaded[:, pl.ds(pl.multiple_of(start, run), run), :] = ref[:, i * run : (i + 1) * run, :]
    sample_run(
        turns[-1][0], tiles, slot_ref, planes_ref, voxel_ref, frac_ref, column_ref, sampled, shaded, None
    )
    rows = out_ref.shape[0]
    row = lax.broadcasted_iota(jnp.int32, (rows, blocks), 0)
    owned = (group_ref[...] >> 2) == (row >> 2)
    chosen = [
        (owned & ((row & (VALUES - 1)) == k)).astype(f32).astype(bf16) for k in range(VALUES)
    ]
    placed = jnp.dot(
        jnp.concatenate(chosen, axis=1),
        shaded[...].reshape(VALUES * blocks, samples),
        preferred_element_type=f32,
    )
    out_ref[...] = placed.astype(bf16)


def sample_last(turns, tiles, blocks_in, group, early, planes):
    blocks, samples = blocks_in[1].shape[1:]
    run = blocks // tiles
    return pl.pallas_call(
        functools.partial(last_kernel, turns, tiles),
        out_shape=jax.ShapeDtypeStruct((GROUPS // SPR * VALUES, samples), bf16),
        in_specs=[whole(pltpu.SMEM)] + [whole(pltpu.VMEM)] * (5 + len(early)),
        out_specs=whole(pltpu.VMEM),
        scratch_shapes=[
            pltpu.VMEM((VALUES, run, samples), f32),
            pltpu.VMEM((VALUES, blocks, samples), bf16),
        ],
        compiler_params=pltpu.CompilerParams(vmem_limit_bytes=8 << 20),
        name="sample_last",
    )(*blocks_in, group, *early, planes)


def composite_kernel(got_ref, background_ref, decode_ref, target_ref, colour_ref, loss_ref):
    rows, rays = got_ref.shape
    got = got_ref[...]
    here = lax.broadcasted_iota(jnp.int32, (rows, rows), 0) // VALUES
    there = lax.broadcasted_iota(jnp.int32, (rows, rows), 1)
    nearer = (there // VALUES < here) & (there % VALUES == VALUES - 1)
    depth = jnp.dot(nearer.astype(f32).astype(bf16), got, preferred_element_type=f32)
    is_depth = lax.broadcasted_iota(jnp.int32, (rows, rays), 0) % VALUES == VALUES - 1
    terms = got.astype(f32) * jnp.where(is_depth, 1.0, jnp.exp(-depth))
    total = jnp.sum(terms.reshape(rows // 8, 8, rays), axis=0)
    total = total + pltpu.roll(total, VALUES, 0)
    behind = jnp.sum(decode_ref[...] * background_ref[...], axis=1, keepdims=True)
    logits = total[0:3] + jnp.exp(-total[3:4]) * behind
    colour = jax.nn.sigmoid(logits)
    difference = colour - target_ref[:, 0, :]
    colour_ref[:, 0, :] = colour
    loss_ref[...] = jnp.sum(difference * difference, axis=0, keepdims=True)


def composite(got, background, decode_weight, target):
    rays = got.shape[1]
    return pl.pallas_call(
        composite_kernel,
        out_shape=(
            jax.ShapeDtypeStruct((3, 1, rays), f32),
            jax.ShapeDtypeStruct((1, rays), f32),
        ),
        in_specs=[whole(pltpu.VMEM)] * 4,
        out_specs=(whole(pltpu.VMEM), whole(pltpu.VMEM)),
        compiler_params=pltpu.CompilerParams(vmem_limit_bytes=8 << 20),
        name="composite",
    )(got, background.reshape(1, -1), decode_weight, target)


def on_device(
    bricks,
    send_list,
    sample_voxel,
    sample_frac,
    block_slot,
    block_group,
    density_weight,
    background,
    decode_weight,
    target,
):
    slab_count = lax.axis_size("slab")
    tiles = lax.axis_size("tile")
    blocks = sample_voxel.shape[1]
    planes = list(decode_bricks(send_list, density_weight, decode_weight, bricks))
    for r in (2, 1, 3):
        planes[r] = lax.ppermute(planes[r], "tile", [(i, (i + r) % tiles) for i in range(tiles)])
    blocks_in = (
        block_slot,
        sample_voxel,
        sample_frac.transpose(0, 2, 1, 3),
        block_group.reshape(blocks, 1),
    )
    turns = ((0,), (1, 3), (2,))
    early = [
        sample_early(turn, tiles, blocks_in, [planes[r] for r in turn]) for turn in turns[:-1]
    ]
    placed = sample_last(turns, tiles, blocks_in, block_group, early, planes[turns[-1][0]])
    placed = placed.reshape(slab_count, VALUES, placed.shape[1])
    got = lax.all_to_all(placed, "slab", split_axis=0, concat_axis=0, tiled=True)
    return composite(got.reshape(-1, got.shape[2]), background, decode_weight, target)


def solution(mesh):
    in_specs = (
        P("slab", "tile", None, None, None),
        P("slab", "tile", None),
        P("slab", "tile", None),
        P("slab", "tile", None, None),
        P("slab", "tile"),
        P("slab", "tile"),
        P(),
        P(),
        P(),
        P(None, "tile", "slab"),
    )
    out_specs = (P(None, "tile", "slab"), P("tile", "slab"))
    return jax.shard_map(
        on_device, mesh=mesh, in_specs=in_specs, out_specs=out_specs, check_vma=False
    )
```

```python
import functools

import jax
import jax.numpy as jnp
from jax import lax
from jax.experimental import pallas as pl
from jax.experimental.pallas import tpu as pltpu
from jax.sharding import PartitionSpec as P

SPR = 4
EDGE = 16
GROUPS = 256
VALUES = 4

step_length = 0.02
f32 = jnp.float32
bf16 = jnp.bfloat16


def whole(space):
    return pl.BlockSpec(memory_space=space)


def decode_kernel(send_ref, density_ref, decode_ref, bricks_ref, *refs):
    tiles = len(refs) - 6
    outs = refs[:tiles]
    send, density, decode, buffer, decoded, sems = refs[tiles:]
    capacity = outs[0].shape[0]
    bricks, channels, edge, plane = bricks_ref.shape[1:]
    small = [
        pltpu.make_async_copy(source, target, sems.at[bricks + i])
        for i, (source, target) in enumerate(
            ((send_ref, send), (density_ref, density), (decode_ref, decode))
        )
    ]
    large = [
        pltpu.make_async_copy(bricks_ref.at[0, brick], buffer.at[brick], sems.at[brick])
        for brick in range(bricks)
    ]
    for copy in small + large:
        copy.start()
    for copy in small:
        copy.wait()

    def one_brick(brick, carry):
        pltpu.make_async_copy(bricks_ref.at[0, brick], buffer.at[brick], sems.at[brick]).wait()
        sums = [jnp.zeros((edge, plane), f32) for _ in range(VALUES)]
        for c in range(channels):
            values = buffer[brick, c].astype(f32)
            weights = [density[c]] + [decode[k, c] for k in range(VALUES - 1)]
            sums = [total + weight * values for total, weight in zip(sums, weights)]
        for k in range(VALUES):
            decoded[brick, k * edge : (k + 1) * edge, :] = sums[k].astype(bf16)
        return carry

    lax.fori_loop(0, bricks, one_brick, 0)
    here = lax.axis_index("tile")
    for r in range(tiles):
        owner = jnp.bitwise_xor(here, r)
        for slot in range(capacity):
            outs[r][slot] = decoded[jnp.clip(send[0, slot, owner], 0, bricks - 1)]


def decode_bricks(send_list, density_weight, decode_weight, bricks):
    tiles, capacity = send_list.shape[1:]
    send_list = send_list.transpose(0, 2, 1)
    count, channels, edge, plane = bricks.shape[1:]
    return pl.pallas_call(
        decode_kernel,
        out_shape=(jax.ShapeDtypeStruct((capacity, VALUES * edge, plane), bf16),) * tiles,
        in_specs=[whole(pltpu.HBM)] * 4,
        out_specs=(whole(pltpu.VMEM),) * tiles,
        scratch_shapes=[
            pltpu.SMEM(send_list.shape, jnp.int32),
            pltpu.SMEM(density_weight.shape, f32),
            pltpu.SMEM(decode_weight.shape, f32),
            pltpu.VMEM((count, channels, edge, plane), bf16),
            pltpu.VMEM((count, VALUES * edge, plane), bf16),
            pltpu.SemaphoreType.DMA((count + 3,)),
        ],
        compiler_params=pltpu.CompilerParams(vmem_limit_bytes=8 << 20),
        name="decode_bricks",
    )(
        *[
            pltpu.with_memory_space_constraint(x, pltpu.HBM)
            for x in (send_list, density_weight, decode_weight, bricks)
        ]
    )


def hat(position, line):
    return jnp.maximum(1.0 - jnp.abs(position - line), 0.0)


def sum_rows(parts):
    row = lax.broadcasted_iota(jnp.int32, parts[0].shape, 0)
    halves = []
    for j in range(4):
        low, high = parts[j], parts[j + 4]
        kept = jnp.where(row < 4, low, high)
        moved = jnp.where(row < 4, high, low)
        both = kept + pltpu.roll(moved, 4, 0)
        both = both + pltpu.roll(both, 1 if j & 1 else 7, 0)
        both = both + pltpu.roll(both, 2 if j & 2 else 6, 0)
        halves.append(both)
    odd = (row & 1) == 1
    pair0 = jnp.where(odd, halves[1], halves[0])
    pair1 = jnp.where(odd, halves[3], halves[2])
    return jnp.where((row & 2) == 2, pair1, pair0)


def every_row(ref, plane, row):
    return ref[plane, pl.ds(row, 8, stride=0), :]


def sample_run(r, tiles, slot_ref, planes_ref, voxel_ref, frac_ref, column_ref, sampled, shaded, base, rows_in, weights_y):
    blocks, samples = voxel_ref.shape[1:]
    capacity = planes_ref.shape[0]
    edge = planes_ref.shape[1] // VALUES
    rays = samples // SPR
    run = blocks // tiles
    batch = 8
    bits = edge.bit_length() - 1
    line = lax.broadcasted_iota(jnp.int32, (8, samples), 0).astype(f32)
    lines = [line + low for low in range(0, edge, 8)]
    turn = jnp.bitwise_xor(lax.axis_index("tile"), r)
    start = turn * run
    lane = lax.broadcasted_iota(jnp.int32, slot_ref.shape, 1)
    second = jnp.where(lane // run == turn, lax.rem(slot_ref[...], capacity) << (lane & (run - 1)), 0)
    second = jnp.sum(second)

    def one_batch(step, carry):
        first = pl.multiple_of(start + step * batch, batch)
        voxel = voxel_ref[0, pl.ds(first, batch), :]
        cells = (voxel >> 2 * bits, (voxel >> bits) & (edge - 1), voxel & (edge - 1))
        buffer = (step & 1) * batch
        for axis, cell in enumerate(cells):
            rows_in[axis, pl.ds(pl.multiple_of(buffer, batch), batch), :] = (
                cell.astype(f32) + frac_ref[0, axis, pl.ds(first, batch), :]
            )
        parts = []
        for j in range(batch):
            at_x, at_y, at_z = [every_row(rows_in, axis, buffer + j) for axis in range(3)]
            weight_x, weight_y, weight_z = [
                [hat(at, low) for low in lines] for at in (at_x, at_y, at_z)
            ]
            weights_y[buffer + j, :8, :] = weight_y[0]
            weights_y[buffer + j, 8:, :] = weight_y[1]
            plane_weights = []
            for y in range(edge):
                row = every_row(weights_y, buffer + j, y)
                plane_weights += [row * weight for weight in weight_z]
            plane_weights = jnp.concatenate(plane_weights, axis=0).astype(bf16)
            slot = (second >> (step * batch + j)) & 1
            sums = jnp.dot(planes_ref[slot], plane_weights, preferred_element_type=f32)
            parts.append(
                [
                    sums[k * edge : k * edge + 8] * weight_x[0]
                    + sums[k * edge + 8 : (k + 1) * edge] * weight_x[1]
                    for k in range(VALUES)
                ]
            )
        place = pl.multiple_of(step * batch, batch)
        for k in range(VALUES):
            sampled[k, pl.ds(place, batch), :] = sum_rows([part[k] for part in parts])
        return carry

    lax.fori_loop(0, run // batch, one_batch, 0, unroll=4)
    quarter = lax.broadcasted_iota(jnp.int32, (run, samples), 1) // rays
    rows = pl.ds(pl.multiple_of(start if base is None else base, run), run)
    logit = sampled[0]
    depth = step_length * (jnp.maximum(logit, 0.0) + jnp.log1p(jnp.exp(-jnp.abs(logit))))
    before = jnp.zeros_like(depth)
    total = depth
    for d in range(1, SPR):
        moved = pltpu.roll(depth, d * rays, 1)
        before = before + jnp.where(quarter >= d, moved, 0.0)
        total = total + moved
    weight = jnp.exp(-before) * (1.0 - jnp.exp(-depth))
    placed = quarter == (column_ref[pl.ds(pl.multiple_of(start, run), run), :] & (SPR - 1))
    for k in range(VALUES - 1):
        value = weight * sampled[k + 1]
        value = value + pltpu.roll(value, 2 * rays, 1)
        value = value + pltpu.roll(value, rays, 1)
        shaded[k, rows, :] = jnp.where(placed, value, 0.0).astype(bf16)
    shaded[VALUES - 1, rows, :] = jnp.where(placed, total, 0.0).astype(bf16)


def weight_scratch(samples):
    return [pltpu.VMEM((3, 16, samples), f32), pltpu.VMEM((16, EDGE, samples), f32)]


def early_kernel(turns, tiles, slot_ref, voxel_ref, frac_ref, column_ref, *refs):
    planes, (out_ref, sampled, *weights) = refs[: len(turns)], refs[len(turns) :]
    run = voxel_ref.shape[1] // tiles
    for i, r in enumerate(turns):
        sample_run(
            r, tiles, slot_ref, planes[i], voxel_ref, frac_ref, column_ref, sampled, out_ref, i * run, *weights
        )


def sample_early(turns, tiles, blocks_in, planes):
    blocks, samples = blocks_in[1].shape[1:]
    run = blocks // tiles
    return pl.pallas_call(
        functools.partial(early_kernel, turns, tiles),
        out_shape=jax.ShapeDtypeStruct((VALUES, len(turns) * run, samples), bf16),
        in_specs=[whole(pltpu.VMEM)] * (4 + len(turns)),
        out_specs=whole(pltpu.VMEM),
        scratch_shapes=[pltpu.VMEM((VALUES, run, samples), f32), *weight_scratch(samples)],
        compiler_params=pltpu.CompilerParams(vmem_limit_bytes=8 << 20),
        name="sample_early",
    )(*blocks_in, *planes)


def last_kernel(turns, tiles, slot_ref, voxel_ref, frac_ref, column_ref, group_ref, *refs):
    early = refs[: len(turns) - 1]
    planes_ref, out_ref, sampled, shaded, *weights = refs[len(turns) - 1 :]
    blocks, samples = voxel_ref.shape[1:]
    run = blocks // tiles
    for done, ref in zip(turns, early):
        for i, r in enumerate(done):
            start = jnp.bitwise_xor(lax.axis_index("tile"), r) * run
            shaded[:, pl.ds(pl.multiple_of(start, run), run), :] = ref[:, i * run : (i + 1) * run, :]
    sample_run(
        turns[-1][0], tiles, slot_ref, planes_ref, voxel_ref, frac_ref, column_ref, sampled, shaded, None, *weights
    )
    rows = out_ref.shape[0]
    row = lax.broadcasted_iota(jnp.int32, (rows, blocks), 0)
    owned = (group_ref[...] >> 2) == (row >> 2)
    chosen = [
        (owned & ((row & (VALUES - 1)) == k)).astype(f32).astype(bf16) for k in range(VALUES)
    ]
    placed = jnp.dot(
        jnp.concatenate(chosen, axis=1),
        shaded[...].reshape(VALUES * blocks, samples),
        preferred_element_type=f32,
    )
    out_ref[...] = placed.astype(bf16)


def sample_last(turns, tiles, blocks_in, group, early, planes):
    blocks, samples = blocks_in[1].shape[1:]
    run = blocks // tiles
    return pl.pallas_call(
        functools.partial(last_kernel, turns, tiles),
        out_shape=jax.ShapeDtypeStruct((GROUPS // SPR * VALUES, samples), bf16),
        in_specs=[whole(pltpu.VMEM)] * (6 + len(early)),
        out_specs=whole(pltpu.VMEM),
        scratch_shapes=[
            pltpu.VMEM((VALUES, run, samples), f32),
            pltpu.VMEM((VALUES, blocks, samples), bf16),
            *weight_scratch(samples),
        ],
        compiler_params=pltpu.CompilerParams(vmem_limit_bytes=8 << 20),
        name="sample_last",
    )(*blocks_in, group, *early, planes)


def composite_kernel(got_ref, background_ref, decode_ref, target_ref, colour_ref, loss_ref):
    rows, rays = got_ref.shape
    got = got_ref[...]
    here = lax.broadcasted_iota(jnp.int32, (rows, rows), 0) // VALUES
    there = lax.broadcasted_iota(jnp.int32, (rows, rows), 1)
    nearer = (there // VALUES < here) & (there % VALUES == VALUES - 1)
    depth = jnp.dot(nearer.astype(f32).astype(bf16), got, preferred_element_type=f32)
    is_depth = lax.broadcasted_iota(jnp.int32, (rows, rays), 0) % VALUES == VALUES - 1
    terms = got.astype(f32) * jnp.where(is_depth, 1.0, jnp.exp(-depth))
    total = jnp.sum(terms.reshape(rows // 8, 8, rays), axis=0)
    total = total + pltpu.roll(total, VALUES, 0)
    behind = jnp.sum(decode_ref[...] * background_ref[...], axis=1, keepdims=True)
    logits = total[0:3] + jnp.exp(-total[3:4]) * behind
    colour = jax.nn.sigmoid(logits)
    difference = colour - target_ref[:, 0, :]
    colour_ref[:, 0, :] = colour
    loss_ref[...] = jnp.sum(difference * difference, axis=0, keepdims=True)


def composite(got, background, decode_weight, target):
    rays = got.shape[1]
    return pl.pallas_call(
        composite_kernel,
        out_shape=(
            jax.ShapeDtypeStruct((3, 1, rays), f32),
            jax.ShapeDtypeStruct((1, rays), f32),
        ),
        in_specs=[whole(pltpu.VMEM)] * 4,
        out_specs=(whole(pltpu.VMEM), whole(pltpu.VMEM)),
        compiler_params=pltpu.CompilerParams(vmem_limit_bytes=8 << 20),
        name="composite",
    )(got, background.reshape(1, -1), decode_weight, target)


def on_device(
    bricks,
    send_list,
    sample_voxel,
    sample_frac,
    block_slot,
    block_group,
    density_weight,
    background,
    decode_weight,
    target,
):
    slab_count = lax.axis_size("slab")
    tiles = lax.axis_size("tile")
    blocks = sample_voxel.shape[1]
    planes = list(decode_bricks(send_list, density_weight, decode_weight, bricks))
    for r in range(1, tiles):
        planes[r] = lax.ppermute(planes[r], "tile", [(i, i ^ r) for i in range(tiles)])
    blocks_in = (
        block_slot,
        sample_voxel,
        sample_frac.transpose(0, 2, 1, 3),
        block_group.reshape(blocks, 1),
    )
    turns = ((0,), (1, 3), (2,))
    early = [
        sample_early(turn, tiles, blocks_in, [planes[r] for r in turn]) for turn in turns[:-1]
    ]
    placed = sample_last(turns, tiles, blocks_in, block_group, early, planes[turns[-1][0]])
    placed = placed.reshape(slab_count, VALUES, placed.shape[1])
    got = lax.all_to_all(placed, "slab", split_axis=0, concat_axis=0, tiled=True)
    return composite(got.reshape(-1, got.shape[2]), background, decode_weight, target)


def solution(mesh):
    in_specs = (
        P("slab", "tile", None, None, None),
        P("slab", "tile", None),
        P("slab", "tile", None),
        P("slab", "tile", None, None),
        P("slab", "tile"),
        P("slab", "tile"),
        P(),
        P(),
        P(),
        P(None, "tile", "slab"),
    )
    out_specs = (P(None, "tile", "slab"), P("tile", "slab"))
    return jax.shard_map(
        on_device, mesh=mesh, in_specs=in_specs, out_specs=out_specs, check_vma=False
    )
```

```python
import functools

import jax
import jax.numpy as jnp
from jax import lax
from jax.experimental import pallas as pl
from jax.experimental.pallas import tpu as pltpu
from jax.sharding import PartitionSpec as P

SPR = 4
EDGE = 16
GROUPS = 256
VALUES = 4

step_length = 0.02
f32 = jnp.float32
bf16 = jnp.bfloat16


def whole(space):
    return pl.BlockSpec(memory_space=space)


def decode_kernel(send_ref, density_ref, decode_ref, bricks_ref, *refs):
    tiles = len(refs) - 9
    outs = refs[:tiles]
    send, density, decode, density_row, decode_rows, buffer, spread, decoded, sems = refs[tiles:]
    capacity = outs[0].shape[0]
    bricks, channels, edge, plane = bricks_ref.shape[1:]
    columns = channels * edge
    half = VALUES * edge
    small = [
        pltpu.make_async_copy(source, target, sems.at[bricks + i])
        for i, (source, target) in enumerate(
            (
                (density_ref, density_row),
                (decode_ref, decode_rows),
                (send_ref, send),
                (density_ref, density),
                (decode_ref, decode),
            )
        )
    ]
    large = [
        pltpu.make_async_copy(bricks_ref.at[0, brick], buffer.at[brick], sems.at[brick])
        for brick in range(bricks)
    ]
    for copy in small + large:
        copy.start()
    for copy in small:
        copy.wait()

    heads = jnp.concatenate([density_row[...], decode_rows[...]], axis=0)
    coarse = heads.astype(bf16)
    fine = (heads - coarse.astype(f32)).astype(bf16)
    repeat = lax.broadcasted_iota(jnp.int32, (channels, columns), 1) // edge == (
        lax.broadcasted_iota(jnp.int32, (channels, columns), 0)
    )
    diagonal = (lax.broadcasted_iota(jnp.int32, (edge, columns), 1) & (edge - 1)) == (
        lax.broadcasted_iota(jnp.int32, (edge, columns), 0)
    )
    for part, term in enumerate((coarse, fine)):
        wide = jnp.dot(term, repeat.astype(f32).astype(bf16), preferred_element_type=f32)
        for k in range(VALUES):
            row = (part * VALUES + k) * edge
            spread[row : row + edge, :] = jnp.where(diagonal, wide[k : k + 1], 0.0).astype(bf16)

    def one_pair(pair, carry):
        for brick in (2 * pair, 2 * pair + 1):
            pltpu.make_async_copy(bricks_ref.at[0, brick], buffer.at[brick], sems.at[brick]).wait()
        both = jnp.dot(
            spread[...], buffer[2 * pair].reshape(columns, plane), preferred_element_type=f32
        )
        decoded[2 * pair] = (both[:half] + both[half:]).astype(bf16)
        sums = [jnp.zeros((edge, plane), f32) for _ in range(VALUES)]
        for c in range(channels):
            values = buffer[2 * pair + 1, c].astype(f32)
            weights = [density[0, c]] + [decode[k, c] for k in range(VALUES - 1)]
            sums = [total + weight * values for total, weight in zip(sums, weights)]
        for k in range(VALUES):
            decoded[2 * pair + 1, k * edge : (k + 1) * edge, :] = sums[k].astype(bf16)
        return carry

    lax.fori_loop(0, bricks // 2, one_pair, 0)
    here = lax.axis_index("tile")
    for r in range(tiles):
        owner = jnp.bitwise_xor(here, r)
        for slot in range(capacity):
            outs[r][slot] = decoded[jnp.clip(send[0, slot, owner], 0, bricks - 1)]


def decode_bricks(send_list, density_weight, decode_weight, bricks):
    tiles, capacity = send_list.shape[1:]
    send_list = send_list.transpose(0, 2, 1)
    count, channels, edge, plane = bricks.shape[1:]
    density_weight = density_weight.reshape(1, channels)
    return pl.pallas_call(
        decode_kernel,
        out_shape=(jax.ShapeDtypeStruct((capacity, VALUES * edge, plane), bf16),) * tiles,
        in_specs=[whole(pltpu.HBM)] * 4,
        out_specs=(whole(pltpu.VMEM),) * tiles,
        scratch_shapes=[
            pltpu.SMEM(send_list.shape, jnp.int32),
            pltpu.SMEM(density_weight.shape, f32),
            pltpu.SMEM(decode_weight.shape, f32),
            pltpu.VMEM(density_weight.shape, f32),
            pltpu.VMEM(decode_weight.shape, f32),
            pltpu.VMEM((count, channels, edge, plane), bf16),
            pltpu.VMEM((2 * VALUES * edge, channels * edge), bf16),
            pltpu.VMEM((count, VALUES * edge, plane), bf16),
            pltpu.SemaphoreType.DMA((count + 5,)),
        ],
        compiler_params=pltpu.CompilerParams(vmem_limit_bytes=8 << 20),
        name="decode_bricks",
    )(
        *[
            pltpu.with_memory_space_constraint(x, pltpu.HBM)
            for x in (send_list, density_weight, decode_weight, bricks)
        ]
    )


def hat(position, line):
    return jnp.maximum(1.0 - jnp.abs(position - line), 0.0)


def sum_rows(parts):
    row = lax.broadcasted_iota(jnp.int32, parts[0].shape, 0)
    halves = []
    for j in range(4):
        low, high = parts[j], parts[j + 4]
        kept = jnp.where(row < 4, low, high)
        moved = jnp.where(row < 4, high, low)
        both = kept + pltpu.roll(moved, 4, 0)
        both = both + pltpu.roll(both, 1 if j & 1 else 7, 0)
        both = both + pltpu.roll(both, 2 if j & 2 else 6, 0)
        halves.append(both)
    odd = (row & 1) == 1
    pair0 = jnp.where(odd, halves[1], halves[0])
    pair1 = jnp.where(odd, halves[3], halves[2])
    return jnp.where((row & 2) == 2, pair1, pair0)


def every_row(ref, plane, row):
    return ref[plane, pl.ds(row, 8, stride=0), :]


def sample_run(r, tiles, slot_ref, planes_ref, voxel_ref, frac_ref, column_ref, sampled, shaded, base, rows_in, weights_y):
    blocks, samples = voxel_ref.shape[1:]
    capacity = planes_ref.shape[0]
    edge = planes_ref.shape[1] // VALUES
    rays = samples // SPR
    run = blocks // tiles
    batch = 8
    bits = edge.bit_length() - 1
    line = lax.broadcasted_iota(jnp.int32, (8, samples), 0).astype(f32)
    lines = [line + low for low in range(0, edge, 8)]
    turn = jnp.bitwise_xor(lax.axis_index("tile"), r)
    start = turn * run
    lane = lax.broadcasted_iota(jnp.int32, slot_ref.shape, 1)
    second = jnp.where(lane // run == turn, lax.rem(slot_ref[...], capacity) << (lane & (run - 1)), 0)
    second = jnp.sum(second)

    def one_batch(step, carry):
        first = pl.multiple_of(start + step * batch, batch)
        voxel = voxel_ref[0, pl.ds(first, batch), :]
        cells = (voxel >> 2 * bits, (voxel >> bits) & (edge - 1), voxel & (edge - 1))
        buffer = (step & 1) * batch
        for axis, cell in enumerate(cells):
            rows_in[axis, pl.ds(pl.multiple_of(buffer, batch), batch), :] = (
                cell.astype(f32) + frac_ref[0, axis, pl.ds(first, batch), :]
            )
        parts = []
        for j in range(batch):
            at_x, at_y, at_z = [every_row(rows_in, axis, buffer + j) for axis in range(3)]
            weight_x, weight_y, weight_z = [
                [hat(at, low) for low in lines] for at in (at_x, at_y, at_z)
            ]
            weights_y[buffer + j, :8, :] = weight_y[0]
            weights_y[buffer + j, 8:, :] = weight_y[1]
            plane_weights = []
            for y in range(edge):
                row = every_row(weights_y, buffer + j, y)
                plane_weights += [row * weight for weight in weight_z]
            plane_weights = jnp.concatenate(plane_weights, axis=0).astype(bf16)
            slot = (second >> (step * batch + j)) & 1
            sums = jnp.dot(planes_ref[slot], plane_weights, preferred_element_type=f32)
            parts.append(
                [
                    sums[k * edge : k * edge + 8] * weight_x[0]
                    + sums[k * edge + 8 : (k + 1) * edge] * weight_x[1]
                    for k in range(VALUES)
                ]
            )
        place = pl.multiple_of(step * batch, batch)
        for k in range(VALUES):
            sampled[k, pl.ds(place, batch), :] = sum_rows([part[k] for part in parts])
        return carry

    lax.fori_loop(0, run // batch, one_batch, 0, unroll=4)
    quarter = lax.broadcasted_iota(jnp.int32, (run, samples), 1) // rays
    rows = pl.ds(pl.multiple_of(start if base is None else base, run), run)
    logit = sampled[0]
    depth = step_length * (jnp.maximum(logit, 0.0) + jnp.log1p(jnp.exp(-jnp.abs(logit))))
    before = jnp.zeros_like(depth)
    total = depth
    for d in range(1, SPR):
        moved = pltpu.roll(depth, d * rays, 1)
        before = before + jnp.where(quarter >= d, moved, 0.0)
        total = total + moved
    weight = jnp.exp(-before) * (1.0 - jnp.exp(-depth))
    placed = quarter == (column_ref[pl.ds(pl.multiple_of(start, run), run), :] & (SPR - 1))
    for k in range(VALUES - 1):
        value = weight * sampled[k + 1]
        value = value + pltpu.roll(value, 2 * rays, 1)
        value = value + pltpu.roll(value, rays, 1)
        shaded[k, rows, :] = jnp.where(placed, value, 0.0).astype(bf16)
    shaded[VALUES - 1, rows, :] = jnp.where(placed, total, 0.0).astype(bf16)


def weight_scratch(samples):
    return [pltpu.VMEM((3, 16, samples), f32), pltpu.VMEM((16, EDGE, samples), f32)]


def early_kernel(turns, tiles, slot_ref, voxel_ref, frac_ref, column_ref, *refs):
    planes, (out_ref, sampled, *weights) = refs[: len(turns)], refs[len(turns) :]
    run = voxel_ref.shape[1] // tiles
    for i, r in enumerate(turns):
        sample_run(
            r, tiles, slot_ref, planes[i], voxel_ref, frac_ref, column_ref, sampled, out_ref, i * run, *weights
        )


def sample_early(turns, tiles, blocks_in, planes):
    blocks, samples = blocks_in[1].shape[1:]
    run = blocks // tiles
    return pl.pallas_call(
        functools.partial(early_kernel, turns, tiles),
        out_shape=jax.ShapeDtypeStruct((VALUES, len(turns) * run, samples), bf16),
        in_specs=[whole(pltpu.VMEM)] * (4 + len(turns)),
        out_specs=whole(pltpu.VMEM),
        scratch_shapes=[pltpu.VMEM((VALUES, run, samples), f32), *weight_scratch(samples)],
        compiler_params=pltpu.CompilerParams(vmem_limit_bytes=8 << 20),
        name="sample_early",
    )(*blocks_in, *planes)


def last_kernel(turns, tiles, slot_ref, voxel_ref, frac_ref, column_ref, group_ref, *refs):
    early = refs[: len(turns) - 1]
    planes_ref, out_ref, sampled, shaded, *weights = refs[len(turns) - 1 :]
    blocks, samples = voxel_ref.shape[1:]
    run = blocks // tiles
    for done, ref in zip(turns, early):
        for i, r in enumerate(done):
            start = jnp.bitwise_xor(lax.axis_index("tile"), r) * run
            shaded[:, pl.ds(pl.multiple_of(start, run), run), :] = ref[:, i * run : (i + 1) * run, :]
    sample_run(
        turns[-1][0], tiles, slot_ref, planes_ref, voxel_ref, frac_ref, column_ref, sampled, shaded, None, *weights
    )
    rows = out_ref.shape[0]
    row = lax.broadcasted_iota(jnp.int32, (rows, blocks), 0)
    owned = (group_ref[...] >> 2) == (row >> 2)
    chosen = [
        (owned & ((row & (VALUES - 1)) == k)).astype(f32).astype(bf16) for k in range(VALUES)
    ]
    placed = jnp.dot(
        jnp.concatenate(chosen, axis=1),
        shaded[...].reshape(VALUES * blocks, samples),
        preferred_element_type=f32,
    )
    out_ref[...] = placed.astype(bf16)


def sample_last(turns, tiles, blocks_in, group, early, planes):
    blocks, samples = blocks_in[1].shape[1:]
    run = blocks // tiles
    return pl.pallas_call(
        functools.partial(last_kernel, turns, tiles),
        out_shape=jax.ShapeDtypeStruct((GROUPS // SPR * VALUES, samples), bf16),
        in_specs=[whole(pltpu.VMEM)] * (6 + len(early)),
        out_specs=whole(pltpu.VMEM),
        scratch_shapes=[
            pltpu.VMEM((VALUES, run, samples), f32),
            pltpu.VMEM((VALUES, blocks, samples), bf16),
            *weight_scratch(samples),
        ],
        compiler_params=pltpu.CompilerParams(vmem_limit_bytes=8 << 20),
        name="sample_last",
    )(*blocks_in, group, *early, planes)


def composite_kernel(got_ref, background_ref, decode_ref, target_ref, colour_ref, loss_ref):
    rows, rays = got_ref.shape
    got = got_ref[...]
    here = lax.broadcasted_iota(jnp.int32, (rows, rows), 0) // VALUES
    there = lax.broadcasted_iota(jnp.int32, (rows, rows), 1)
    nearer = (there // VALUES < here) & (there % VALUES == VALUES - 1)
    depth = jnp.dot(nearer.astype(f32).astype(bf16), got, preferred_element_type=f32)
    is_depth = lax.broadcasted_iota(jnp.int32, (rows, rays), 0) % VALUES == VALUES - 1
    terms = got.astype(f32) * jnp.where(is_depth, 1.0, jnp.exp(-depth))
    total = jnp.sum(terms.reshape(rows // 8, 8, rays), axis=0)
    total = total + pltpu.roll(total, VALUES, 0)
    behind = jnp.sum(decode_ref[...] * background_ref[...], axis=1, keepdims=True)
    logits = total[0:3] + jnp.exp(-total[3:4]) * behind
    colour = jax.nn.sigmoid(logits)
    difference = colour - target_ref[:, 0, :]
    colour_ref[:, 0, :] = colour
    loss_ref[...] = jnp.sum(difference * difference, axis=0, keepdims=True)


def composite(got, background, decode_weight, target):
    rays = got.shape[1]
    return pl.pallas_call(
        composite_kernel,
        out_shape=(
            jax.ShapeDtypeStruct((3, 1, rays), f32),
            jax.ShapeDtypeStruct((1, rays), f32),
        ),
        in_specs=[whole(pltpu.VMEM)] * 4,
        out_specs=(whole(pltpu.VMEM), whole(pltpu.VMEM)),
        compiler_params=pltpu.CompilerParams(vmem_limit_bytes=8 << 20),
        name="composite",
    )(got, background.reshape(1, -1), decode_weight, target)


def on_device(
    bricks,
    send_list,
    sample_voxel,
    sample_frac,
    block_slot,
    block_group,
    density_weight,
    background,
    decode_weight,
    target,
):
    slab_count = lax.axis_size("slab")
    tiles = lax.axis_size("tile")
    blocks = sample_voxel.shape[1]
    planes = list(decode_bricks(send_list, density_weight, decode_weight, bricks))
    for r in range(1, tiles):
        planes[r] = lax.ppermute(planes[r], "tile", [(i, i ^ r) for i in range(tiles)])
    blocks_in = (
        block_slot,
        sample_voxel,
        sample_frac.transpose(0, 2, 1, 3),
        block_group.reshape(blocks, 1),
    )
    turns = ((0,), (1, 3), (2,))
    early = [
        sample_early(turn, tiles, blocks_in, [planes[r] for r in turn]) for turn in turns[:-1]
    ]
    placed = sample_last(turns, tiles, blocks_in, block_group, early, planes[turns[-1][0]])
    placed = placed.reshape(slab_count, VALUES, placed.shape[1])
    got = lax.all_to_all(placed, "slab", split_axis=0, concat_axis=0, tiled=True)
    return composite(got.reshape(-1, got.shape[2]), background, decode_weight, target)


def solution(mesh):
    in_specs = (
        P("slab", "tile", None, None, None),
        P("slab", "tile", None),
        P("slab", "tile", None),
        P("slab", "tile", None, None),
        P("slab", "tile"),
        P("slab", "tile"),
        P(),
        P(),
        P(),
        P(None, "tile", "slab"),
    )
    out_specs = (P(None, "tile", "slab"), P("tile", "slab"))
    return jax.shard_map(
        on_device, mesh=mesh, in_specs=in_specs, out_specs=out_specs, check_vma=False
    )
```

```python
import functools

import jax
import jax.numpy as jnp
from jax import lax
from jax.experimental import pallas as pl
from jax.experimental.pallas import tpu as pltpu
from jax.sharding import PartitionSpec as P


SPR = 4
EDGE = 16
ORDER = (3, 1, 2)
TURNS = ((0, 3), (1,), (2,))
GROUPS = 256
VALUES = 4

step_length = 0.02
f32 = jnp.float32
bf16 = jnp.bfloat16


def whole(space):
    return pl.BlockSpec(memory_space=space)


def decode_kernel(send_ref, density_ref, decode_ref, bricks_ref, *refs):
    tiles = len(refs) - 9
    outs = refs[:tiles]
    send, density, decode, density_row, decode_rows, buffer, spread, decoded, sems = refs[tiles:]
    capacity = outs[0].shape[0]
    bricks, channels, edge, plane = bricks_ref.shape[1:]
    columns = channels * edge
    half = VALUES * edge
    small = [
        pltpu.make_async_copy(source, target, sems.at[bricks + i])
        for i, (source, target) in enumerate(
            (
                (density_ref, density_row),
                (decode_ref, decode_rows),
                (send_ref, send),
                (density_ref, density),
                (decode_ref, decode),
            )
        )
    ]
    large = [
        pltpu.make_async_copy(bricks_ref.at[0, brick], buffer.at[brick], sems.at[brick])
        for brick in range(bricks)
    ]
    for copy in small + large:
        copy.start()
    for copy in small:
        copy.wait()

    heads = jnp.concatenate([density_row[...], decode_rows[...]], axis=0)
    coarse = heads.astype(bf16)
    fine = (heads - coarse.astype(f32)).astype(bf16)
    repeat = lax.broadcasted_iota(jnp.int32, (channels, columns), 1) // edge == (
        lax.broadcasted_iota(jnp.int32, (channels, columns), 0)
    )
    diagonal = (lax.broadcasted_iota(jnp.int32, (edge, columns), 1) & (edge - 1)) == (
        lax.broadcasted_iota(jnp.int32, (edge, columns), 0)
    )
    for part, term in enumerate((coarse, fine)):
        wide = jnp.dot(term, repeat.astype(f32).astype(bf16), preferred_element_type=f32)
        for k in range(VALUES):
            row = (part * VALUES + k) * edge
            spread[row : row + edge, :] = jnp.where(diagonal, wide[k : k + 1], 0.0).astype(bf16)

    def one_pair(pair, carry):
        for brick in (2 * pair, 2 * pair + 1):
            pltpu.make_async_copy(bricks_ref.at[0, brick], buffer.at[brick], sems.at[brick]).wait()
        both = jnp.dot(
            spread[...], buffer[2 * pair].reshape(columns, plane), preferred_element_type=f32
        )
        decoded[2 * pair] = (both[:half] + both[half:]).astype(bf16)
        sums = [jnp.zeros((edge, plane), f32) for _ in range(VALUES)]
        for c in range(channels):
            values = buffer[2 * pair + 1, c].astype(f32)
            weights = [density[0, c]] + [decode[k, c] for k in range(VALUES - 1)]
            sums = [total + weight * values for total, weight in zip(sums, weights)]
        for k in range(VALUES):
            decoded[2 * pair + 1, k * edge : (k + 1) * edge, :] = sums[k].astype(bf16)
        return carry

    lax.fori_loop(0, bricks // 2, one_pair, 0)
    here = lax.axis_index("tile")
    for r in range(tiles):
        owner = jnp.bitwise_xor(here, r)
        for slot in range(capacity):
            outs[r][slot] = decoded[jnp.clip(send[0, slot, owner], 0, bricks - 1)]


def decode_bricks(send_list, density_weight, decode_weight, bricks):
    tiles, capacity = send_list.shape[1:]
    send_list = send_list.transpose(0, 2, 1)
    count, channels, edge, plane = bricks.shape[1:]
    density_weight = density_weight.reshape(1, channels)
    return pl.pallas_call(
        decode_kernel,
        out_shape=(jax.ShapeDtypeStruct((capacity, VALUES * edge, plane), bf16),) * tiles,
        in_specs=[whole(pltpu.HBM)] * 4,
        out_specs=(whole(pltpu.VMEM),) * tiles,
        scratch_shapes=[
            pltpu.SMEM(send_list.shape, jnp.int32),
            pltpu.SMEM(density_weight.shape, f32),
            pltpu.SMEM(decode_weight.shape, f32),
            pltpu.VMEM(density_weight.shape, f32),
            pltpu.VMEM(decode_weight.shape, f32),
            pltpu.VMEM((count, channels, edge, plane), bf16),
            pltpu.VMEM((2 * VALUES * edge, channels * edge), bf16),
            pltpu.VMEM((count, VALUES * edge, plane), bf16),
            pltpu.SemaphoreType.DMA((count + 5,)),
        ],
        compiler_params=pltpu.CompilerParams(vmem_limit_bytes=8 << 20),
        name="decode_bricks",
    )(
        *[
            pltpu.with_memory_space_constraint(x, pltpu.HBM)
            for x in (send_list, density_weight, decode_weight, bricks)
        ]
    )


def hat(position, line):
    return jnp.maximum(1.0 - jnp.abs(position - line), 0.0)


def sum_rows(parts):
    row = lax.broadcasted_iota(jnp.int32, parts[0].shape, 0)
    halves = []
    for j in range(4):
        low, high = parts[j], parts[j + 4]
        kept = jnp.where(row < 4, low, high)
        moved = jnp.where(row < 4, high, low)
        both = kept + pltpu.roll(moved, 4, 0)
        both = both + pltpu.roll(both, 1 if j & 1 else 7, 0)
        both = both + pltpu.roll(both, 2 if j & 2 else 6, 0)
        halves.append(both)
    odd = (row & 1) == 1
    pair0 = jnp.where(odd, halves[1], halves[0])
    pair1 = jnp.where(odd, halves[3], halves[2])
    return jnp.where((row & 2) == 2, pair1, pair0)


def every_row(ref, plane, row):
    return ref[plane, pl.ds(row, 8, stride=0), :]


def sample_run(r, tiles, slot_ref, planes_ref, voxel_ref, frac_ref, column_ref, sampled, shaded, base, rows_in, weights_y):
    blocks, samples = voxel_ref.shape[1:]
    capacity = planes_ref.shape[0]
    edge = planes_ref.shape[1] // VALUES
    rays = samples // SPR
    run = blocks // tiles
    batch = 8
    bits = edge.bit_length() - 1
    line = lax.broadcasted_iota(jnp.int32, (8, samples), 0).astype(f32)
    lines = [line + low for low in range(0, edge, 8)]
    turn = jnp.bitwise_xor(lax.axis_index("tile"), r)
    start = turn * run
    lane = lax.broadcasted_iota(jnp.int32, slot_ref.shape, 1)
    second = jnp.where(lane // run == turn, lax.rem(slot_ref[...], capacity) << (lane & (run - 1)), 0)
    second = jnp.sum(second)

    def one_batch(step, carry):
        first = pl.multiple_of(start + step * batch, batch)
        voxel = voxel_ref[0, pl.ds(first, batch), :]
        cells = (voxel >> 2 * bits, (voxel >> bits) & (edge - 1), voxel & (edge - 1))
        buffer = (step & 1) * batch
        for axis, cell in enumerate(cells):
            rows_in[axis, pl.ds(pl.multiple_of(buffer, batch), batch), :] = (
                cell.astype(f32) + frac_ref[0, axis, pl.ds(first, batch), :]
            )
        parts = []
        for j in range(batch):
            at_x, at_y, at_z = [every_row(rows_in, axis, buffer + j) for axis in range(3)]
            weight_x, weight_y, weight_z = [
                [hat(at, low) for low in lines] for at in (at_x, at_y, at_z)
            ]
            weights_y[buffer + j, :8, :] = weight_y[0]
            weights_y[buffer + j, 8:, :] = weight_y[1]
            plane_weights = []
            for y in range(edge):
                row = every_row(weights_y, buffer + j, y)
                plane_weights += [row * weight for weight in weight_z]
            plane_weights = jnp.concatenate(plane_weights, axis=0).astype(bf16)
            slot = (second >> (step * batch + j)) & 1
            sums = jnp.dot(planes_ref[slot], plane_weights, preferred_element_type=f32)
            parts.append(
                [
                    sums[k * edge : k * edge + 8] * weight_x[0]
                    + sums[k * edge + 8 : (k + 1) * edge] * weight_x[1]
                    for k in range(VALUES)
                ]
            )
        place = pl.multiple_of(step * batch, batch)
        for k in range(VALUES):
            sampled[k, pl.ds(place, batch), :] = sum_rows([part[k] for part in parts])
        return carry

    lax.fori_loop(0, run // batch, one_batch, 0, unroll=4)
    quarter = lax.broadcasted_iota(jnp.int32, (run, samples), 1) // rays
    rows = pl.ds(pl.multiple_of(start if base is None else base, run), run)
    logit = sampled[0]
    depth = step_length * (jnp.maximum(logit, 0.0) + jnp.log1p(jnp.exp(-jnp.abs(logit))))
    before = jnp.zeros_like(depth)
    total = depth
    for d in range(1, SPR):
        moved = pltpu.roll(depth, d * rays, 1)
        before = before + jnp.where(quarter >= d, moved, 0.0)
        total = total + moved
    weight = jnp.exp(-before) * (1.0 - jnp.exp(-depth))
    placed = quarter == (column_ref[pl.ds(pl.multiple_of(start, run), run), :] & (SPR - 1))
    for k in range(VALUES - 1):
        value = weight * sampled[k + 1]
        value = value + pltpu.roll(value, 2 * rays, 1)
        value = value + pltpu.roll(value, rays, 1)
        shaded[k, rows, :] = jnp.where(placed, value, 0.0).astype(bf16)
    shaded[VALUES - 1, rows, :] = jnp.where(placed, total, 0.0).astype(bf16)


def weight_scratch(samples):
    return [pltpu.VMEM((3, 16, samples), f32), pltpu.VMEM((16, EDGE, samples), f32)]


def early_kernel(turns, tiles, slot_ref, voxel_ref, frac_ref, column_ref, *refs):
    planes, (out_ref, sampled, *weights) = refs[: len(turns)], refs[-4:]
    run = voxel_ref.shape[1] // tiles
    for i, r in enumerate(turns):
        sample_run(
            r, tiles, slot_ref, planes[i], voxel_ref, frac_ref, column_ref, sampled, out_ref, i * run, *weights
        )


def sample_early(turns, tiles, blocks_in, planes, before):
    blocks, samples = blocks_in[1].shape[1:]
    run = blocks // tiles
    return pl.pallas_call(
        functools.partial(early_kernel, turns, tiles),
        out_shape=jax.ShapeDtypeStruct((VALUES, len(turns) * run, samples), bf16),
        in_specs=[whole(pltpu.VMEM)] * (4 + len(turns)) + [whole(pl.ANY)] * len(before),
        out_specs=whole(pltpu.VMEM),
        scratch_shapes=[pltpu.VMEM((VALUES, run, samples), f32), *weight_scratch(samples)],
        compiler_params=pltpu.CompilerParams(vmem_limit_bytes=8 << 20),
        name="sample_early",
    )(*blocks_in, *planes, *before)


def last_kernel(turns, tiles, slot_ref, voxel_ref, frac_ref, column_ref, group_ref, *refs):
    early = refs[: len(turns) - 1]
    planes_ref, out_ref, sampled, shaded, *weights = refs[len(turns) - 1 :]
    blocks, samples = voxel_ref.shape[1:]
    run = blocks // tiles
    for done, ref in zip(turns, early):
        for i, r in enumerate(done):
            start = jnp.bitwise_xor(lax.axis_index("tile"), r) * run
            shaded[:, pl.ds(pl.multiple_of(start, run), run), :] = ref[:, i * run : (i + 1) * run, :]
    sample_run(
        turns[-1][0], tiles, slot_ref, planes_ref, voxel_ref, frac_ref, column_ref, sampled, shaded, None, *weights
    )
    rows = out_ref.shape[0]
    row = lax.broadcasted_iota(jnp.int32, (rows, blocks), 0)
    owned = (group_ref[...] >> 2) == (row >> 2)
    chosen = [
        (owned & ((row & (VALUES - 1)) == k)).astype(f32).astype(bf16) for k in range(VALUES)
    ]
    placed = jnp.dot(
        jnp.concatenate(chosen, axis=1),
        shaded[...].reshape(VALUES * blocks, samples),
        preferred_element_type=f32,
    )
    out_ref[...] = placed.astype(bf16)


def sample_last(turns, tiles, blocks_in, group, early, planes):
    blocks, samples = blocks_in[1].shape[1:]
    run = blocks // tiles
    return pl.pallas_call(
        functools.partial(last_kernel, turns, tiles),
        out_shape=jax.ShapeDtypeStruct((GROUPS // SPR * VALUES, samples), bf16),
        in_specs=[whole(pltpu.VMEM)] * (6 + len(early)),
        out_specs=whole(pltpu.VMEM),
        scratch_shapes=[
            pltpu.VMEM((VALUES, run, samples), f32),
            pltpu.VMEM((VALUES, blocks, samples), bf16),
            *weight_scratch(samples),
        ],
        compiler_params=pltpu.CompilerParams(vmem_limit_bytes=8 << 20),
        name="sample_last",
    )(*blocks_in, group, *early, planes)


def composite_kernel(got_ref, background_ref, decode_ref, target_ref, colour_ref, loss_ref):
    rows, rays = got_ref.shape
    got = got_ref[...]
    here = lax.broadcasted_iota(jnp.int32, (rows, rows), 0) // VALUES
    there = lax.broadcasted_iota(jnp.int32, (rows, rows), 1)
    nearer = (there // VALUES < here) & (there % VALUES == VALUES - 1)
    depth = jnp.dot(nearer.astype(f32).astype(bf16), got, preferred_element_type=f32)
    is_depth = lax.broadcasted_iota(jnp.int32, (rows, rays), 0) % VALUES == VALUES - 1
    terms = got.astype(f32) * jnp.where(is_depth, 1.0, jnp.exp(-depth))
    total = jnp.sum(terms.reshape(rows // 8, 8, rays), axis=0)
    total = total + pltpu.roll(total, VALUES, 0)
    behind = jnp.sum(decode_ref[...] * background_ref[...], axis=1, keepdims=True)
    logits = total[0:3] + jnp.exp(-total[3:4]) * behind
    colour = jax.nn.sigmoid(logits)
    difference = colour - target_ref[:, 0, :]
    colour_ref[:, 0, :] = colour
    loss_ref[...] = jnp.sum(difference * difference, axis=0, keepdims=True)


def composite(got, background, decode_weight, target):
    rays = got.shape[1]
    return pl.pallas_call(
        composite_kernel,
        out_shape=(
            jax.ShapeDtypeStruct((3, 1, rays), f32),
            jax.ShapeDtypeStruct((1, rays), f32),
        ),
        in_specs=[whole(pltpu.VMEM)] * 4,
        out_specs=(whole(pltpu.VMEM), whole(pltpu.VMEM)),
        compiler_params=pltpu.CompilerParams(vmem_limit_bytes=8 << 20),
        name="composite",
    )(got, background.reshape(1, -1), decode_weight, target)


def stages(
    bricks,
    send_list,
    sample_voxel,
    sample_frac,
    block_slot,
    block_group,
    density_weight,
    background,
    decode_weight,
    target,
):
    slab_count = lax.axis_size("slab")
    tiles = lax.axis_size("tile")
    blocks = sample_voxel.shape[1]
    planes = list(decode_bricks(send_list, density_weight, decode_weight, bricks))
    for r in ORDER:
        planes[r] = lax.ppermute(planes[r], "tile", [(i, i ^ r) for i in range(tiles)])
    blocks_in = (
        block_slot,
        sample_voxel,
        sample_frac.transpose(0, 2, 1, 3),
        block_group.reshape(blocks, 1),
    )
    turns = TURNS
    early = []
    for turn in turns[:-1]:
        early.append(sample_early(turn, tiles, blocks_in, [planes[r] for r in turn], early[-1:]))
    placed = sample_last(turns, tiles, blocks_in, block_group, early, planes[turns[-1][0]])
    placed = placed.reshape(slab_count, VALUES, placed.shape[1])
    got = lax.all_to_all(placed, "slab", split_axis=0, concat_axis=0, tiled=True)
    return composite(got.reshape(-1, got.shape[2]), background, decode_weight, target)


def solution(mesh):
    in_specs = (
        P("slab", "tile", None, None, None),
        P("slab", "tile", None),
        P("slab", "tile", None),
        P("slab", "tile", None, None),
        P("slab", "tile"),
        P("slab", "tile"),
        P(),
        P(),
        P(),
        P(None, "tile", "slab"),
    )
    out_specs = (P(None, "tile", "slab"), P("tile", "slab"))
    return jax.shard_map(stages, mesh=mesh, in_specs=in_specs, out_specs=out_specs, check_vma=False)
```
